32 devices in a mesh: dp: 2 (over y), ctx: 4 (over z), tp: 4 (over x, core).
Axes of the slice: x: 2, y: 2, z: 4, core: 2. Of those that a mesh axis runs over, the one named last changes fastest.
Arguments:
- tokens: bfloat16 [2, 4096, 768], P('dp', ('ctx', 'tp')), may hold values from -6 to 6
- enc_states: bfloat16 [2, 4096, 768], P('dp', 'ctx'), may hold values from -6 to 6
- chosen_blocks: int32 [2, 4096, 8], P('dp'), may hold values from 0 to 31, as said below
- seq_lengths: int32 [2], P('dp'), may hold values from 1024 to 4096, as said below
- cotangent: bfloat16 [2, 4096, 768], P('dp', ('ctx', 'tp')), may hold values from -6 to 6
- self_query: bfloat16 [768, 768], P(('dp', 'ctx'), 'tp'), may hold values from -0.21875 to 0.21875
- self_key: bfloat16 [768, 768], P(('dp', 'ctx'), 'tp'), may hold values from -0.21875 to 0.21875
- self_value: bfloat16 [768, 768], P(('dp', 'ctx'), 'tp'), may hold values from -0.21875 to 0.21875
- self_output: bfloat16 [768, 768], P(('dp', 'ctx'), 'tp'), may hold values from -6 to 6
- cross_query: bfloat16 [768, 768], P(('dp', 'ctx'), 'tp'), may hold values from -0.21875 to 0.21875
- cross_key: bfloat16 [768, 768], P(('dp', 'ctx'), 'tp'), may hold values from -0.21875 to 0.21875
- cross_value: bfloat16 [768, 768], P(('dp', 'ctx'), 'tp'), may hold values from -0.21875 to 0.21875
- cross_output: bfloat16 [768, 768], P(('dp', 'ctx'), 'tp'), may hold values from -4 to 4
- ffn_inner: bfloat16 [768, 3072], P(('dp', 'ctx'), 'tp'), may hold values from -0.21875 to 0.21875
- ffn_outer: bfloat16 [768, 3072], P(('dp', 'ctx'), 'tp'), may hold values from -0.109375 to 0.109375
- query_bias: float32 [768], P(('dp', 'ctx', 'tp')), may hold values from -3 to 3
- value_bias: float32 [768], P(('dp', 'ctx', 'tp')), may hold values from -3 to 3
- output_bias: float32 [768], P(('dp', 'ctx', 'tp')), may hold values from -3 to 3
- cquery_bias: float32 [768], P(('dp', 'ctx', 'tp')), may hold values from -3 to 3
- cvalue_bias: float32 [768], P(('dp', 'ctx', 'tp')), may hold values from -3 to 3
- coutput_bias: float32 [768], P(('dp', 'ctx', 'tp')), may hold values from -3 to 3
- inner_bias: float32 [3072], P(('dp', 'ctx', 'tp')), may hold values from -3 to 3
- outer_bias: float32 [768], P(('dp', 'ctx', 'tp')), may hold values from -3 to 3
- norm1_gain: float32 [768], P(('dp', 'ctx', 'tp')), may hold values from 0.1 to 1.9
- norm1_shift: float32 [768], P(('dp', 'ctx', 'tp')), may hold values from -2 to 2
- norm2_gain: float32 [768], P(('dp', 'ctx', 'tp')), may hold values from 0.1 to 1.9
- norm2_shift: float32 [768], P(('dp', 'ctx', 'tp')), may hold values from -2 to 2
- norm3_gain: float32 [768], P(('dp', 'ctx', 'tp')), may hold values from 0.1 to 1.9
- norm3_shift: float32 [768], P(('dp', 'ctx', 'tp')), may hold values from -2 to 2
Outputs:
- output: bfloat16 [2, 4096, 768], P('dp', ('ctx', 'tp'))
- token_grad: bfloat16 [2, 4096, 768], P('dp', ('ctx', 'tp'))
- state_grad: bfloat16 [2, 4096, 768], P('dp', ('ctx', 'tp'))
- self_query_grad: float32 [768, 768], P(('dp', 'ctx'), 'tp')
- self_key_grad: float32 [768, 768], P(('dp', 'ctx'), 'tp')
- self_value_grad: float32 [768, 768], P(('dp', 'ctx'), 'tp')
- self_output_grad: float32 [768, 768], P(('dp', 'ctx'), 'tp')
- cross_query_grad: float32 [768, 768], P(('dp', 'ctx'), 'tp')
- cross_key_grad: float32 [768, 768], P(('dp', 'ctx'), 'tp')
- cross_value_grad: float32 [768, 768], P(('dp', 'ctx'), 'tp')
- cross_output_grad: float32 [768, 768], P(('dp', 'ctx'), 'tp')
- ffn_inner_grad: float32 [768, 3072], P(('dp', 'ctx'), 'tp')
- ffn_outer_grad: float32 [768, 3072], P(('dp', 'ctx'), 'tp')
- query_bias_grad: float32 [768], P(('dp', 'ctx', 'tp'))
- value_bias_grad: float32 [768], P(('dp', 'ctx', 'tp'))
- output_bias_grad: float32 [768], P(('dp', 'ctx', 'tp'))
- cquery_bias_grad: float32 [768], P(('dp', 'ctx', 'tp'))
- cvalue_bias_grad: float32 [768], P(('dp', 'ctx', 'tp'))
- coutput_bias_grad: float32 [768], P(('dp', 'ctx', 'tp'))
- inner_bias_grad: float32 [3072], P(('dp', 'ctx', 'tp'))
- outer_bias_grad: float32 [768], P(('dp', 'ctx', 'tp'))
- norm1_gain_grad: float32 [768], P(('dp', 'ctx', 'tp'))
- norm1_shift_grad: float32 [768], P(('dp', 'ctx', 'tp'))
- norm2_gain_grad: float32 [768], P(('dp', 'ctx', 'tp'))
- norm2_shift_grad: float32 [768], P(('dp', 'ctx', 'tp'))
- norm3_gain_grad: float32 [768], P(('dp', 'ctx', 'tp'))
- norm3_shift_grad: float32 [768], P(('dp', 'ctx', 'tp'))
The draws below stay inside these ranges and needn't reach their ends.
Inputs may be any that keep to these rules, and one draw needn't show every extreme that they name: `seq_lengths`: slots at or beyond a sequence's length are padding; in every draw some sequence has the full 4096 slots. `chosen_blocks`: the 8 block ids of one query are distinct; block b is encoder rows b * 128 to (b + 1) * 128 - 1 of the query's own sequence.
All inputs are finite; a program needn't handle non-finite values.
Results may differ from the reference program's by a relative error of at most 0.028.
Values may be sent and summed in bfloat16 or wider, within the bound.
No kernel may reach another device: no remote copies, remote signals or barrier semaphores. Data moves between devices by JAX's collectives and lax.ppermute only.
A program may use at most 192 MiB of HBM per device.

```python
import jax
import jax.numpy as jnp
from jax import lax

D = 768
HEADS = 12
HD = 64
FF = 3072
BLK = 128
SEL = 8
SEQ_LEN = 4096
SEQS = 2
ENC = 4096
NBLK = 32


def draw_seq_lengths(key, part):
    drawn = jax.random.randint(key, (SEQS,), SEQ_LEN // 4, SEQ_LEN + 1)
    longest = jax.random.randint(jax.random.fold_in(key, 7), (), 0, SEQS)
    return jnp.where(jnp.arange(SEQS) == longest, SEQ_LEN, drawn).astype(jnp.int32)


def draw_chosen_blocks(key, part):
    scores = jax.random.randint(key, (SEQS, SEQ_LEN, NBLK), 0, 2 ** 20) * NBLK + jnp.arange(NBLK)
    picked = lax.top_k(scores, SEL)[1]
    return picked.astype(jnp.int32)


def shard_levels(rng, extent, cuts, smallest, top_value):
    level, own = 1.0, jax.random.fold_in(rng, 6)
    for axis_at, parts in cuts:
        heights = jnp.exp(jax.random.uniform(jax.random.fold_in(own, axis_at), (parts,), jnp.float32, smallest / len(cuts), top_value / len(cuts)))
        level = level * jnp.repeat(heights, extent[axis_at] // parts).reshape([-1 if axis == axis_at else 1 for axis in range(len(extent))])
    return level


def noise(key, extent, scale, bound, cuts=(), dtype=jnp.bfloat16):
    result = scale * jax.random.normal(key, extent, jnp.float32)
    if cuts:
        result = result * shard_levels(key, extent, cuts, -0.22, 0.18)
    return jnp.clip(result, -bound, bound).astype(dtype)


def setup_inputs(seed: int = 0) -> dict:
    key_of = jax.random.split(jax.random.key(seed), 30)
    tokens = noise(key_of[0], (SEQS, SEQ_LEN, D), 1.0, 6.0, ((0, 2), (1, 16)))
    enc_states = noise(key_of[1], (SEQS, ENC, D), 1.0, 6.0, ((0, 2), (1, 4)))
    chosen_blocks = draw_chosen_blocks(jax.random.fold_in(key_of[29], 71), 0)
    seq_lengths = draw_seq_lengths(jax.random.fold_in(key_of[29], 71), 0)
    cotangent = noise(key_of[4], (SEQS, SEQ_LEN, D), 1.0, 6.0, ((0, 2), (1, 16)))
    self_query = noise(key_of[5], (D, D), D ** -0.5, 0.21875, ((0, 8), (1, 4)))
    self_key = noise(key_of[6], (D, D), D ** -0.5, 0.21875, ((0, 8), (1, 4)))
    self_value = noise(key_of[7], (D, D), D ** -0.5, 0.21875, ((0, 8), (1, 4)))
    self_output = noise(key_of[8], (D, D), 1 ** -0.5, 6.0, ((0, 8), (1, 4)))
    cross_query = noise(key_of[9], (D, D), D ** -0.5, 0.21875, ((0, 8), (1, 4)))
    cross_key = noise(key_of[10], (D, D), D ** -0.5, 0.21875, ((0, 8), (1, 4)))
    cross_value = noise(key_of[11], (D, D), D ** -0.5, 0.21875, ((0, 8), (1, 4)))
    cross_output = noise(key_of[12], (D, D), 2 ** -0.5, 4.0, ((0, 8), (1, 4)))
    ffn_inner = noise(key_of[13], (D, FF), D ** -0.5, 0.21875, ((0, 8), (1, 4)))
    ffn_outer = noise(key_of[14], (D, FF), FF ** -0.5, 0.109375, ((0, 8), (1, 4)))
    query_bias = noise(key_of[15], (D,), 0.5, 3.0, ((0, 32),), jnp.float32)
    value_bias = noise(key_of[16], (D,), 0.5, 3.0, ((0, 32),), jnp.float32)
    output_bias = noise(key_of[17], (D,), 0.5, 3.0, ((0, 32),), jnp.float32)
    cquery_bias = noise(key_of[18], (D,), 0.5, 3.0, ((0, 32),), jnp.float32)
    cvalue_bias = noise(key_of[19], (D,), 0.5, 3.0, ((0, 32),), jnp.float32)
    coutput_bias = noise(key_of[20], (D,), 0.5, 3.0, ((0, 32),), jnp.float32)
    inner_bias = noise(key_of[21], (FF,), 0.5, 3.0, ((0, 32),), jnp.float32)
    outer_bias = noise(key_of[22], (D,), 0.5, 3.0, ((0, 32),), jnp.float32)
    norm1_gain = jnp.clip(1.0 + 0.18 * jax.random.normal(key_of[23], (D,), jnp.float32), 0.1, 1.9)
    norm1_shift = noise(key_of[24], (D,), 0.3, 2.0, ((0, 32),), jnp.float32)
    norm2_gain = jnp.clip(1.0 + 0.18 * jax.random.normal(key_of[25], (D,), jnp.float32), 0.1, 1.9)
    norm2_shift = noise(key_of[26], (D,), 0.3, 2.0, ((0, 32),), jnp.float32)
    norm3_gain = jnp.clip(1.0 + 0.18 * jax.random.normal(key_of[27], (D,), jnp.float32), 0.1, 1.9)
    norm3_shift = noise(key_of[28], (D,), 0.3, 2.0, ((0, 32),), jnp.float32)
    return {"tokens": tokens, "enc_states": enc_states, "chosen_blocks": chosen_blocks, "seq_lengths": seq_lengths, "cotangent": cotangent, "self_query": self_query, "self_key": self_key, "self_value": self_value, "self_output": self_output, "cross_query": cross_query, "cross_key": cross_key, "cross_value": cross_value, "cross_output": cross_output, "ffn_inner": ffn_inner, "ffn_outer": ffn_outer, "query_bias": query_bias, "value_bias": value_bias, "output_bias": output_bias, "cquery_bias": cquery_bias, "cvalue_bias": cvalue_bias, "coutput_bias": coutput_bias, "inner_bias": inner_bias, "outer_bias": outer_bias, "norm1_gain": norm1_gain, "norm1_shift": norm1_shift, "norm2_gain": norm2_gain, "norm2_shift": norm2_shift, "norm3_gain": norm3_gain, "norm3_shift": norm3_shift}


@jax.custom_vjp
def low(v):
    return lax.optimization_barrier(v.astype(jnp.bfloat16)).astype(jnp.float32)

@jax.custom_vjp
def low_back(v):
    return v

def low_keep(v):
    return (low(v), None)

def low_pass(kept, grad):
    return (grad,)

def back_keep(v):
    return (v, None)

def back_low(kept, grad):
    return (low(grad),)
low.defvjp(low_keep, low_pass)
low_back.defvjp(back_keep, back_low)
masked_fill = -1e+30
norm_eps = 1e-05

def both_round(value):
    return low_back(low(value))

def matmul_high(left, right):
    return jnp.dot(left, right, precision=lax.Precision.HIGHEST)

def layer_norm(residual, norm_gain, norm_shift):
    average = lax.optimization_barrier(jnp.mean(residual, axis=-1, keepdims=True))
    centred = residual - average
    variance = lax.optimization_barrier(jnp.mean(centred * centred, axis=-1, keepdims=True))
    return centred * lax.rsqrt(variance + norm_eps) * norm_gain + norm_shift

def split_heads(matrix):
    return matrix.reshape(matrix.shape[0], HEADS, HD)

def attention(query_heads, key_heads, value_heads, allowed_fn, block_rows):
    block_total = query_heads.shape[0] // block_rows
    query_blocks = query_heads.reshape((block_total, block_rows) + query_heads.shape[1:])

    def one_block(inputs):
        block_query, block_number = inputs
        scores = jnp.einsum('qhd,khd->hqk', block_query, key_heads, precision=lax.Precision.HIGHEST)
        scores = low_back(jnp.where(allowed_fn(block_number)[None], scores, masked_fill))
        weights = jax.nn.softmax(scores, axis=-1)
        return jnp.einsum('hqk,khd->qhd', low(weights), value_heads, precision=lax.Precision.HIGHEST)
    mixed = lax.map(jax.checkpoint(one_block), (query_blocks, jnp.arange(block_total)))
    return mixed.reshape(query_heads.shape)

def sequence_forward(inputs, param_set, vector_set):
    token_rows, state_rows, chosen, length = inputs
    self_query, self_key, self_value, self_output, cross_query, cross_key, cross_value, cross_output, ffn_inner, ffn_outer = param_set
    query_bias, value_bias, output_bias, cquery_bias, cvalue_bias, coutput_bias, inner_bias, outer_bias, norm1_gain, norm1_shift, norm2_gain, norm2_shift, norm3_gain, norm3_shift = vector_set
    positions = jnp.arange(SEQ_LEN)
    row_valid = (positions < length).astype(jnp.float32)
    block_rows = min(512, SEQ_LEN)
    self_queries = both_round((matmul_high(token_rows, self_query) + query_bias) * 0.125)
    self_keys = both_round(matmul_high(token_rows, self_key))
    self_values = both_round(matmul_high(token_rows, self_value) + value_bias)

    def self_allowed(block_number):
        block_pos = block_number * block_rows + jnp.arange(block_rows)
        return (positions[None, :] <= block_pos[:, None]) & (positions[None, :] < length)
    self_mixed = attention(split_heads(self_queries), split_heads(self_keys), split_heads(self_values), self_allowed, block_rows)
    self_mixed = both_round(self_mixed.reshape(SEQ_LEN, D))
    branch_one = low_back(matmul_high(self_mixed, self_output.T))
    hidden_one = layer_norm(token_rows + branch_one + output_bias, norm1_gain, norm1_shift)
    low_one = low(hidden_one)
    cross_queries = both_round((matmul_high(low_one, cross_query) + cquery_bias) * 0.125)
    enc_keys = both_round(matmul_high(state_rows, cross_key))
    enc_values = both_round(matmul_high(state_rows, cross_value) + cvalue_bias)
    block_ids = jnp.arange(NBLK)

    def cross_allowed(block_number):
        picked = lax.dynamic_slice_in_dim(chosen, (block_number * block_rows).astype(jnp.int32), block_rows, 0)
        block_hit = jnp.any(picked[:, :, None] == block_ids[None, None, :], axis=1)
        return jnp.broadcast_to(block_hit[:, :, None], (block_rows, NBLK, BLK)).reshape(block_rows, ENC)
    cross_mixed = attention(split_heads(cross_queries), split_heads(enc_keys), split_heads(enc_values), cross_allowed, block_rows)
    cross_mixed = both_round(cross_mixed.reshape(SEQ_LEN, D))
    branch_two = low_back(matmul_high(cross_mixed, cross_output.T))
    hidden_two = layer_norm(hidden_one + branch_two + coutput_bias, norm2_gain, norm2_shift)
    low_two = low(hidden_two)
    inner_pre = low_back(matmul_high(low_two, ffn_inner) + inner_bias)
    activated = low(jax.nn.gelu(inner_pre, approximate=False))
    branch_three = low_back(matmul_high(activated, ffn_outer.T))
    hidden_three = layer_norm(hidden_two + branch_three + outer_bias, norm3_gain, norm3_shift)
    return hidden_three * row_valid[:, None]

def reference(tokens, enc_states, chosen_blocks, seq_lengths, cotangent, self_query, self_key, self_value, self_output, cross_query, cross_key, cross_value, cross_output, ffn_inner, ffn_outer, query_bias, value_bias, output_bias, cquery_bias, cvalue_bias, coutput_bias, inner_bias, outer_bias, norm1_gain, norm1_shift, norm2_gain, norm2_shift, norm3_gain, norm3_shift):
    param_set = tuple((matrix.astype(jnp.float32) for matrix in (self_query, self_key, self_value, self_output, cross_query, cross_key, cross_value, cross_output, ffn_inner, ffn_outer)))
    vector_set = (query_bias, value_bias, output_bias, cquery_bias, cvalue_bias, coutput_bias, inner_bias, outer_bias, norm1_gain, norm1_shift, norm2_gain, norm2_shift, norm3_gain, norm3_shift)

    def forward(token_all, state_all, params_now, vectors_now):

        def one_sequence(inputs):
            return sequence_forward(inputs, params_now, vectors_now)
        return lax.map(one_sequence, (token_all, state_all, chosen_blocks, seq_lengths))
    output, pullback = jax.vjp(forward, tokens.astype(jnp.float32), enc_states.astype(jnp.float32), param_set, vector_set)
    token_grad, state_grad, param_grads, vector_grads = pullback(cotangent.astype(jnp.float32))
    gq_self, gk_self, gv_self, go_self, gq_cross, gk_cross, gv_cross, go_cross, g_inner, g_outer = param_grads
    gb_query, gb_value, gb_output, gb_cquery, gb_cvalue, gb_coutput, gb_inner, gb_outer, gn_gain1, gn_shift1, gn_gain2, gn_shift2, gn_gain3, gn_shift3 = vector_grads
    return (output.astype(jnp.bfloat16), token_grad.astype(jnp.bfloat16), state_grad.astype(jnp.bfloat16), gq_self, gk_self, gv_self, go_self, gq_cross, gk_cross, gv_cross, go_cross, g_inner, g_outer, gb_query, gb_value, gb_output, gb_cquery, gb_cvalue, gb_coutput, gb_inner, gb_outer, gn_gain1, gn_shift1, gn_gain2, gn_shift2, gn_gain3, gn_shift3)
```

```python
import functools

import jax
import jax.numpy as jnp
from jax import lax
from jax.experimental import pallas as pl
from jax.experimental.pallas import tpu as pltpu
from jax.sharding import PartitionSpec as P

HD = 64
BLK = 128
QB = 256
KT = 512

masked_fill = -1e30
norm_eps = 1e-05
bf16 = jnp.bfloat16
f32 = jnp.float32


def layer_norm(residual, norm_gain, norm_shift):
    average = jnp.mean(residual, axis=-1, keepdims=True)
    centred = residual - average
    variance = jnp.mean(centred * centred, axis=-1, keepdims=True)
    return centred * lax.rsqrt(variance + norm_eps) * norm_gain + norm_shift


def exact_gelu(inner_pre):
    return jax.nn.gelu(inner_pre, approximate=False)


def matmul(left, right):
    return jnp.dot(left, right, preferred_element_type=f32)


def matmul_nt(left, right):
    return lax.dot_general(left, right, (((1,), (1,)), ((), ())), preferred_element_type=f32)


def matmul_tn(left, right):
    return lax.dot_general(left, right, (((0,), (0,)), ((), ())), preferred_element_type=f32)


def matmul_tt(left, right):
    return lax.dot_general(left, right, (((0,), (1,)), ((), ())), preferred_element_type=f32)


def swap(x, axis, mask):
    size = lax.axis_size(axis)
    return lax.ppermute(x, axis, [(i, i ^ mask) for i in range(size)])


def bits_of(size):
    assert size & (size - 1) == 0
    return [1 << b for b in range(size.bit_length() - 1)]


def gather_axis(x, axis, masks=None):
    index = lax.axis_index(axis)
    out = x[None]
    for mask in masks or bits_of(lax.axis_size(axis)):
        other = swap(out, axis, mask)
        low = (index & mask) == 0
        out = jnp.concatenate([jnp.where(low, out, other), jnp.where(low, other, out)], axis=0)
    return out


def tp_gather(x):
    index = lax.axis_index("tp")
    rows, width = x.shape
    far = swap(x, "tp", 2)
    low = (index & 2) == 0
    pair = jnp.stack([jnp.where(low, x, far), jnp.where(low, far, x)])
    near = swap(pair, "tp", 1)
    low = (index & 1) == 0
    both = jnp.stack([jnp.where(low, pair, near), jnp.where(low, near, pair)], axis=1)
    return both.reshape(4 * rows, width)


def tp_scatter(left, right_t, contract):
    index = lax.axis_index("tp")
    near, far = index & 1, index >> 1
    rows = left.shape[0] // 4
    split = left.reshape(2, 2, rows, left.shape[1])

    def part(which):
        lhs = lax.dynamic_index_in_dim(split, which, axis=1, keepdims=False)
        return contract(lhs.reshape(2 * rows, left.shape[1]), right_t).reshape(2, rows, -1)

    sent = swap(part(1 - near).astype(bf16), "tp", 1)
    kept = part(near) + sent.astype(f32)
    away = lax.dynamic_index_in_dim(kept, 1 - far, axis=0, keepdims=False)
    home = lax.dynamic_index_in_dim(kept, far, axis=0, keepdims=False)
    return home + swap(away.astype(bf16), "tp", 2).astype(f32)


def head_keep(width, head):
    lane = lax.broadcasted_iota(jnp.int32, (1, width), 1)
    return lane, (lane >= head * HD) & (lane < head * HD + HD)


def causal_bound(scal_ref, row, tile, tiles_per_group, group_rows):
    group = scal_ref[0]
    rel = tile // tiles_per_group
    base = (group - rel) * group_rows + (tile - rel * tiles_per_group) * KT
    kpos = base + lax.broadcasted_iota(jnp.int32, (QB, KT), 1)
    qpos = group * group_rows + row * QB + lax.broadcasted_iota(jnp.int32, (QB, KT), 0)
    return (kpos <= qpos) & (kpos < scal_ref[1])


def attend_kernel(cfg, scal_ref, q_ref, k_ref, v_ref, o_ref, lse_ref, s_scr):
    heads, tiles, causal, group_rows, kcols, vcols, vlow = cfg
    width = q_ref.shape[1]
    count = (scal_ref[0] + 1) * (group_rows // KT) if causal else tiles
    lane_w = lax.broadcasted_iota(jnp.int32, (1, width), 1)

    def row_body(row, carry):
        rows = pl.ds(pl.multiple_of(row * QB, QB), QB)
        q_all = q_ref[rows, :]
        out = jnp.zeros((QB, heads * HD), f32)
        lse_out = jnp.zeros((QB, 128), f32)
        for head in range(heads):
            keep = ((lane_w >= head * HD) & (lane_w < head * HD + HD)) | (lane_w >= heads * HD)
            q_h = q_all * keep.astype(bf16)

            def scores(tile, top):
                k_t = k_ref[pl.ds(pl.multiple_of(tile * KT, KT), KT), kcols[0] : kcols[1]]
                s = matmul_nt(q_h, k_t)
                if causal:
                    allowed = causal_bound(scal_ref, row, tile, group_rows // KT, group_rows)
                    s = jnp.where(allowed, s, masked_fill)
                s_scr[tile] = s
                for c in range(KT // 128):
                    top = jnp.maximum(top, s[:, c * 128 : (c + 1) * 128])
                return top

            top = lax.fori_loop(0, count, scores, jnp.full((QB, 128), masked_fill, f32))
            row_max = jnp.max(top, axis=1, keepdims=True)

            def mix(tile, state):
                total, acc = state
                p = jnp.exp(s_scr[tile] - row_max)
                for c in range(KT // 128):
                    total = total + p[:, c * 128 : (c + 1) * 128]
                v_t = v_ref[pl.ds(pl.multiple_of(tile * KT, KT), KT), vcols[0] : vcols[1]]
                return total, acc + matmul(p.astype(bf16), v_t)

            total, acc = lax.fori_loop(
                0,
                count,
                mix,
                (jnp.zeros((QB, 128), f32), jnp.zeros((QB, vcols[1] - vcols[0]), f32)),
            )
            row_sum = jnp.sum(total, axis=1, keepdims=True)
            _, keep_o = head_keep(heads * HD, head)
            out = jnp.where(keep_o, acc[:, vlow:] / row_sum, out)
            lane = lax.broadcasted_iota(jnp.int32, (1, 128), 1)
            lse_out = jnp.where(lane == head, row_max + jnp.log(row_sum), lse_out)
        o_ref[rows, :] = out
        lse_ref[rows, :] = lse_out
        return carry

    lax.fori_loop(0, q_ref.shape[0] // QB, row_body, 0)


def attend_grad_kernel(
    cfg, scal_ref, q_ref, k_ref, v_ref, do_ref, o_ref, lse_ref, qt_ref, dot_ref,
    dq_ref, dkv_ref, dk_scr, dv_scr,
):
    heads, tiles, causal, group_rows, kcols, vcols, vlow = cfg
    width = q_ref.shape[1]
    count = (scal_ref[0] + 1) * (group_rows // KT) if causal else tiles
    lane_w = lax.broadcasted_iota(jnp.int32, (1, width), 1)
    dk_scr[...] = jnp.zeros(dk_scr.shape, f32)
    dv_scr[...] = jnp.zeros(dv_scr.shape, f32)
    span = heads * HD

    def row_body(row, carry):
        rows = pl.ds(pl.multiple_of(row * QB, QB), QB)
        q_all = q_ref[rows, :]
        do_all = do_ref[rows, :]
        prod = do_all[:, vlow:].astype(f32) * o_ref[rows, :]
        lse_all = lse_ref[rows, :]
        dq_out = jnp.zeros((QB, span), f32)
        for head in range(heads):
            keep = ((lane_w >= head * HD) & (lane_w < head * HD + HD)) | (lane_w >= span)
            q_h = q_all * keep.astype(bf16)
            lane_v = lax.broadcasted_iota(jnp.int32, (1, vlow + span), 1)
            keep_v = (lane_v >= vlow + head * HD) & (lane_v < vlow + head * HD + HD)
            do_h = do_all * keep_v.astype(bf16)
            _, keep_o = head_keep(span, head)
            delta = jnp.sum(jnp.where(keep_o, prod, 0.0), axis=1, keepdims=True)
            lse = lse_all[:, head : head + 1]
            qt = qt_ref[row, head * HD : (head + 1) * HD, :]
            dot_t = dot_ref[row, head * HD : (head + 1) * HD, :]

            def step(tile, acc):
                at = pl.ds(pl.multiple_of(tile * KT, KT), KT)
                k_t = k_ref[at, kcols[0] : kcols[1]]
                v_t = v_ref[at, vcols[0] : vcols[1]]
                s = matmul_nt(q_h, k_t)
                if causal:
                    allowed = causal_bound(scal_ref, row, tile, group_rows // KT, group_rows)
                    s = jnp.where(allowed, s, masked_fill)
                p = jnp.exp(s - lse)
                ds = (p * (matmul_nt(do_h, v_t) - delta)).astype(bf16)
                dv_scr[tile, head * HD : (head + 1) * HD, :] += matmul(dot_t, p.astype(bf16))
                dk_scr[tile, head * HD : (head + 1) * HD, :] += matmul(qt, ds)
                return acc + matmul(ds, k_t)

            acc = lax.fori_loop(0, count, step, jnp.zeros((QB, kcols[1] - kcols[0]), f32))
            dq_out = jnp.where(keep_o, acc[:, :span], dq_out)
        dq_ref[rows, :] = dq_out.astype(bf16)
        return carry

    lax.fori_loop(0, q_ref.shape[0] // QB, row_body, 0)
    per = group_rows // KT
    for tile in range(tiles):
        cols = pl.ds((tile % per) * KT, KT)
        dkv_ref[tile // per, 0:span, cols] = dk_scr[tile].astype(bf16)
        dkv_ref[tile // per, span : 2 * span, cols] = dv_scr[tile].astype(bf16)


def smem():
    return pl.BlockSpec(memory_space=pltpu.SMEM)


def vmem():
    return pl.BlockSpec(memory_space=pltpu.VMEM)


def attend(cfg, scal, q, k, v):
    heads, tiles = cfg[0], cfg[1]
    rows = q.shape[0]
    return pl.pallas_call(
        functools.partial(attend_kernel, cfg),
        out_shape=(
            jax.ShapeDtypeStruct((rows, heads * HD), f32),
            jax.ShapeDtypeStruct((rows, 128), f32),
        ),
        in_specs=[smem(), vmem(), vmem(), vmem()],
        out_specs=(vmem(), vmem()),
        scratch_shapes=[pltpu.VMEM((tiles, QB, KT), f32)],
        name="attend",
    )(scal, q, k, v)


def row_blocks_t(x):
    return x.reshape(x.shape[0] // QB, QB, x.shape[1]).swapaxes(1, 2)


def attend_grad(cfg, scal, q, k, v, do, o, lse):
    heads, tiles, _, group_rows, _, _, vlow = cfg
    rows, span = q.shape[0], heads * HD
    do_wide = jnp.pad(do, ((0, 0), (vlow, 0))) if vlow else do
    groups = tiles * KT // group_rows
    return pl.pallas_call(
        functools.partial(attend_grad_kernel, cfg),
        out_shape=(
            jax.ShapeDtypeStruct((rows, span), bf16),
            jax.ShapeDtypeStruct((groups, 2 * span, group_rows), bf16),
        ),
        in_specs=[smem()] + [vmem()] * 8,
        out_specs=(vmem(), vmem()),
        scratch_shapes=[pltpu.VMEM((tiles, span, KT), f32), pltpu.VMEM((tiles, span, KT), f32)],
        name="attend_grad",
    )(scal, q, k, v, do_wide, o, lse, row_blocks_t(q[:, :span]), row_blocks_t(do))


def per_device(
    tokens,
    enc_states,
    chosen_blocks,
    seq_lengths,
    cotangent,
    self_query,
    self_key,
    self_value,
    self_output,
    cross_query,
    cross_key,
    cross_value,
    cross_output,
    ffn_inner,
    ffn_outer,
    query_bias,
    value_bias,
    output_bias,
    cquery_bias,
    cvalue_bias,
    coutput_bias,
    inner_bias,
    outer_bias,
    norm1_gain,
    norm1_shift,
    norm2_gain,
    norm2_shift,
    norm3_gain,
    norm3_shift,
):
    tp_count = lax.axis_size("tp")
    ctx_count = lax.axis_size("ctx")
    dp_count = lax.axis_size("dp")
    head_slot = lax.axis_index("tp")
    group_slot = lax.axis_index("ctx")
    assert tp_count == 4
    columns = self_query.shape[1]
    hidden_cols = ffn_inner.shape[1]
    heads = columns // HD
    both = 2 * columns

    def gather_weights(*parts):
        return lax.all_gather(
            jnp.concatenate(parts, axis=1), ("dp", "ctx"), axis=0, tiled=True
        )

    self_full = gather_weights(self_key, self_value, self_query, self_output)
    cross_full = gather_weights(cross_key, cross_value, cross_query, cross_output)
    ffn_full = gather_weights(ffn_inner, ffn_outer)
    skv_full, query_full, output_full = (
        self_full[:, :both],
        self_full[:, both : 3 * columns],
        self_full[:, 3 * columns :],
    )
    ckv_full, cquery_full, coutput_full = (
        cross_full[:, :both],
        cross_full[:, both : 3 * columns],
        cross_full[:, 3 * columns :],
    )
    inner_full, outer_full = ffn_full[:, :hidden_cols], ffn_full[:, hidden_cols:]

    vectors = (
        query_bias, value_bias, output_bias, cquery_bias, cvalue_bias, coutput_bias, inner_bias,
        outer_bias, norm1_gain, norm1_shift, norm2_gain, norm2_shift, norm3_gain, norm3_shift,
    )
    sizes = [vector.shape[0] for vector in vectors]
    packed = jnp.concatenate(vectors)
    packed_size = packed.shape[0]
    members = dp_count * ctx_count * tp_count
    spread = packed[None, :]
    spread = gather_axis(spread, "tp", [1, 2])
    spread = gather_axis(spread.reshape(1, tp_count, packed_size), "ctx")
    spread = gather_axis(spread.reshape(1, ctx_count * tp_count, packed_size), "dp")
    spread = spread.reshape(members, packed_size)
    full_vectors = []
    at = 0
    for size in sizes:
        full_vectors.append(spread[:, at : at + size].reshape(members * size))
        at += size
    (
        query_vec, value_vec, output_vec, cquery_vec, cvalue_vec, coutput_vec, inner_vec,
        outer_vec, gain_one, shift_one, gain_two, shift_two, gain_three, shift_three,
    ) = full_vectors

    def local_cols(vector, width):
        return lax.dynamic_slice_in_dim(vector, head_slot * width, width, 0)

    def placed(local_sum, full_width):
        return lax.dynamic_update_slice_in_dim(
            jnp.zeros((full_width,), f32), local_sum, head_slot * local_sum.shape[0], 0
        )

    def value_half(vector):
        return jnp.concatenate([jnp.zeros((columns,), f32), local_cols(vector, columns)])

    token_rows = tokens[0]
    own_rows, width = token_rows.shape
    group_rows = own_rows * tp_count
    seq_total = group_rows * ctx_count
    enc_group = enc_states.shape[1]
    enc_total = enc_group * ctx_count
    length = seq_lengths[0]
    own_pos = group_slot * group_rows + head_slot * own_rows + jnp.arange(own_rows)
    row_valid = (own_pos < length).astype(f32)[:, None]
    scal = jnp.stack([group_slot.astype(jnp.int32), length.astype(jnp.int32)])

    self_cfg = (heads, seq_total // KT, True, group_rows, (0, columns), (columns - HD, both), HD)
    complete_rows = tp_gather(token_rows)
    self_kv = (matmul(complete_rows, skv_full) + value_half(value_vec)).astype(bf16)
    self_queries = (
        (matmul(complete_rows, query_full) + local_cols(query_vec, columns)) * 0.125
    ).astype(bf16)
    right = [(i, i + 1) for i in range(ctx_count - 1)]
    left = [(i + 1, i) for i in range(ctx_count - 1)]
    held, stack = self_kv, [self_kv]
    for _ in range(ctx_count - 1):
        held = lax.ppermute(held, "ctx", right)
        stack.append(held)
    kv_rel = jnp.concatenate(stack, axis=0)

    state_rows = enc_states[0]
    enc_kv = (matmul(state_rows, ckv_full) + value_half(cvalue_vec)).astype(bf16)
    all_enc_kv = lax.all_gather(enc_kv, "ctx", axis=0, tiled=True)
    block_count = enc_total // BLK
    block_of = lax.broadcasted_iota(jnp.int32, (enc_total, block_count), 0) // BLK
    hot = (block_of == lax.broadcasted_iota(jnp.int32, (enc_total, block_count), 1)).astype(bf16)
    spare = -(columns + block_count) % 128
    enc_k = jnp.concatenate(
        [all_enc_kv[:, :columns], hot, jnp.zeros((enc_total, spare), bf16)], axis=1
    )
    enc_v = all_enc_kv[:, columns:]
    picked = lax.dynamic_slice_in_dim(chosen_blocks[0], group_slot * group_rows, group_rows, 0)
    hit = jnp.any(picked[:, :, None] == jnp.arange(block_count)[None, None, :], axis=1)
    block_fill = jnp.where(hit, 0.0, masked_fill).astype(bf16)
    cross_width = columns + block_count + spare
    cross_cfg = (heads, enc_total // KT, False, enc_group, (0, cross_width), (0, columns), 0)

    self_mix, self_lse = attend(self_cfg, scal, self_queries, kv_rel, kv_rel)
    self_mixed = self_mix.astype(bf16)
    resid_one = (
        token_rows.astype(f32) + tp_scatter(self_mixed, output_full, matmul_nt) + output_vec
    )
    hidden_one, pull_one = jax.vjp(layer_norm, resid_one, gain_one, shift_one)
    rows_one = tp_gather(hidden_one.astype(bf16))
    cross_queries = (
        (matmul(rows_one, cquery_full) + local_cols(cquery_vec, columns)) * 0.125
    ).astype(bf16)
    cross_q = jnp.concatenate(
        [cross_queries, block_fill, jnp.zeros((group_rows, spare), bf16)], axis=1
    )
    cross_mix, cross_lse = attend(cross_cfg, scal, cross_q, enc_k, enc_v)
    cross_mixed = cross_mix.astype(bf16)
    resid_two = hidden_one + tp_scatter(cross_mixed, coutput_full, matmul_nt) + coutput_vec
    hidden_two, pull_two = jax.vjp(layer_norm, resid_two, gain_two, shift_two)
    rows_two = tp_gather(hidden_two.astype(bf16))
    inner_pre = matmul(rows_two, inner_full) + local_cols(inner_vec, hidden_cols)
    activated_full, pull_gelu = jax.vjp(exact_gelu, inner_pre)
    activated = activated_full.astype(bf16)
    resid_three = hidden_two + tp_scatter(activated, outer_full, matmul_nt) + outer_vec
    hidden_three, pull_three = jax.vjp(layer_norm, resid_three, gain_three, shift_three)
    output = (hidden_three * row_valid).astype(bf16)

    def scatter_weights(*parts):
        return lax.psum_scatter(
            jnp.concatenate([part.astype(bf16) for part in parts], axis=1),
            ("dp", "ctx"),
            scatter_dimension=0,
            tiled=True,
        ).astype(f32)

    grad_resid3, grad_gain3, grad_shift3 = pull_three(cotangent[0].astype(f32) * row_valid)
    ffn_grad_rows = tp_gather(grad_resid3.astype(bf16))
    act_grad = matmul(ffn_grad_rows, outer_full)
    (inner_grad_full,) = pull_gelu(act_grad)
    inner_grad = inner_grad_full.astype(bf16)
    grad_hidden2 = grad_resid3 + tp_scatter(inner_grad, inner_full, matmul_nt)
    ffn_part = scatter_weights(
        matmul_tn(rows_two, inner_grad), matmul_tn(ffn_grad_rows, activated)
    )
    inner_bgrad = placed(jnp.sum(inner_grad, axis=0, dtype=f32), inner_vec.shape[0])
    outer_bgrad = jnp.sum(grad_resid3, axis=0)
    grad_resid2, grad_gain2, grad_shift2 = pull_two(grad_hidden2)
    cross_grad_rows = tp_gather(grad_resid2.astype(bf16))
    cross_mixed_grad = matmul(cross_grad_rows, coutput_full).astype(bf16)
    coutput_bgrad = jnp.sum(grad_resid2, axis=0)
    cross_query_grad, cross_kv_part = attend_grad(
        cross_cfg, scal, cross_q, enc_k, enc_v, cross_mixed_grad, cross_mix, cross_lse
    )
    grad_hidden1 = grad_resid2 + tp_scatter(
        cross_query_grad, cquery_full, lambda a, b: 0.125 * matmul_nt(a, b)
    )
    enc_grad_t = lax.psum_scatter(cross_kv_part, "ctx", scatter_dimension=0, tiled=False)
    cross_part = scatter_weights(
        matmul_tt(state_rows, enc_grad_t),
        0.125 * matmul_tn(rows_one, cross_query_grad),
        matmul_tn(cross_grad_rows, cross_mixed),
    )
    cquery_bgrad = placed(0.125 * jnp.sum(cross_query_grad, axis=0, dtype=f32), width)
    cvalue_bgrad = placed(jnp.sum(enc_grad_t[columns:], axis=1, dtype=f32), width)
    state_grad = tp_scatter(enc_grad_t.T, ckv_full, matmul_nt).astype(bf16)
    grad_resid1, grad_gain1, grad_shift1 = pull_one(grad_hidden1)
    self_grad_rows = tp_gather(grad_resid1.astype(bf16))
    self_mixed_grad = matmul(self_grad_rows, output_full).astype(bf16)
    output_bgrad = jnp.sum(grad_resid1, axis=0)
    squery_grad, self_kv_part = attend_grad(
        self_cfg, scal, self_queries, kv_rel, kv_rel, self_mixed_grad, self_mix, self_lse
    )
    moved = lax.ppermute(self_kv_part[ctx_count - 1], "ctx", left)
    for rel in range(ctx_count - 2, 0, -1):
        moved = lax.ppermute(
            (self_kv_part[rel].astype(f32) + moved.astype(f32)).astype(bf16), "ctx", left
        )
    self_grad_t = (self_kv_part[0].astype(f32) + moved.astype(f32)).astype(bf16)
    self_part = scatter_weights(
        matmul_tt(complete_rows, self_grad_t),
        0.125 * matmul_tn(complete_rows, squery_grad),
        matmul_tn(self_grad_rows, self_mixed),
    )
    query_bgrad = placed(0.125 * jnp.sum(squery_grad, axis=0, dtype=f32), width)
    value_bgrad = placed(jnp.sum(self_grad_t[columns:], axis=1, dtype=f32), width)
    kvq_grad = jnp.concatenate([self_grad_t.T, (squery_grad * 0.125).astype(bf16)], axis=1)
    token_grad = grad_resid1 + tp_scatter(kvq_grad, self_full[:, : 3 * columns], matmul_nt)

    vector_sums = (
        query_bgrad, value_bgrad, output_bgrad, cquery_bgrad, cvalue_bgrad, coutput_bgrad,
        inner_bgrad, outer_bgrad, grad_gain1, grad_shift1, grad_gain2, grad_shift2, grad_gain3,
        grad_shift3,
    )
    folded = jnp.concatenate(
        [vector.reshape(members, size) for vector, size in zip(vector_sums, sizes)], axis=1
    )
    for axis in ("dp", "ctx", "tp"):
        index = lax.axis_index(axis)
        for mask in reversed(bits_of(lax.axis_size(axis))):
            halves = folded.reshape(2, folded.shape[0] // 2, packed_size)
            bit = (index & mask) != 0
            home = jnp.where(bit, halves[1], halves[0])
            away = jnp.where(bit, halves[0], halves[1])
            folded = home + swap(away, axis, mask)
    own_vectors = folded.reshape(packed_size)
    vector_grads = []
    at = 0
    for size in sizes:
        vector_grads.append(own_vectors[at : at + size])
        at += size

    def cols(part, start, stop):
        return part[:, start * columns : stop * columns]

    weight_grads = (
        cols(self_part, 2, 3), cols(self_part, 0, 1), cols(self_part, 1, 2), cols(self_part, 3, 4),
        cols(cross_part, 2, 3), cols(cross_part, 0, 1), cols(cross_part, 1, 2),
        cols(cross_part, 3, 4), ffn_part[:, :hidden_cols], ffn_part[:, hidden_cols:],
    )
    return (
        (output[None], token_grad.astype(bf16)[None], state_grad[None])
        + weight_grads
        + tuple(vector_grads)
    )


def solution(mesh):
    in_specs = (
        P("dp", ("ctx", "tp"), None),
        P("dp", "ctx", None),
        P("dp", None, None),
        P("dp"),
        P("dp", ("ctx", "tp"), None),
        P(("dp", "ctx"), "tp"),
        P(("dp", "ctx"), "tp"),
        P(("dp", "ctx"), "tp"),
        P(("dp", "ctx"), "tp"),
        P(("dp", "ctx"), "tp"),
        P(("dp", "ctx"), "tp"),
        P(("dp", "ctx"), "tp"),
        P(("dp", "ctx"), "tp"),
        P(("dp", "ctx"), "tp"),
        P(("dp", "ctx"), "tp"),
        P(("dp", "ctx", "tp")),
        P(("dp", "ctx", "tp")),
        P(("dp", "ctx", "tp")),
        P(("dp", "ctx", "tp")),
        P(("dp", "ctx", "tp")),
        P(("dp", "ctx", "tp")),
        P(("dp", "ctx", "tp")),
        P(("dp", "ctx", "tp")),
        P(("dp", "ctx", "tp")),
        P(("dp", "ctx", "tp")),
        P(("dp", "ctx", "tp")),
        P(("dp", "ctx", "tp")),
        P(("dp", "ctx", "tp")),
        P(("dp", "ctx", "tp")),
    )
    out_specs = (
        P("dp", ("ctx", "tp"), None),
        P("dp", ("ctx", "tp"), None),
        P("dp", ("ctx", "tp"), None),
        P(("dp", "ctx"), "tp"),
        P(("dp", "ctx"), "tp"),
        P(("dp", "ctx"), "tp"),
        P(("dp", "ctx"), "tp"),
        P(("dp", "ctx"), "tp"),
        P(("dp", "ctx"), "tp"),
        P(("dp", "ctx"), "tp"),
        P(("dp", "ctx"), "tp"),
        P(("dp", "ctx"), "tp"),
        P(("dp", "ctx"), "tp"),
        P(("dp", "ctx", "tp")),
        P(("dp", "ctx", "tp")),
        P(("dp", "ctx", "tp")),
        P(("dp", "ctx", "tp")),
        P(("dp", "ctx", "tp")),
        P(("dp", "ctx", "tp")),
        P(("dp", "ctx", "tp")),
        P(("dp", "ctx", "tp")),
        P(("dp", "ctx", "tp")),
        P(("dp", "ctx", "tp")),
        P(("dp", "ctx", "tp")),
        P(("dp", "ctx", "tp")),
        P(("dp", "ctx", "tp")),
        P(("dp", "ctx", "tp")),
    )
    return jax.shard_map(
        per_device, mesh=mesh, in_specs=in_specs, out_specs=out_specs, check_vma=False
    )
```

```python
import functools

import jax
import jax.numpy as jnp
from jax import lax
from jax.experimental import pallas as pl
from jax.experimental.pallas import tpu as pltpu
from jax.sharding import PartitionSpec as P

HD = 64
BLK = 128
FQ = 256
GQ = 512
WIDE = 256

masked_fill = -1e30
norm_eps = 1e-05
bf16 = jnp.bfloat16
f32 = jnp.float32


def layer_norm(residual, norm_gain, norm_shift):
    average = jnp.mean(residual, axis=-1, keepdims=True)
    centred = residual - average
    variance = jnp.mean(centred * centred, axis=-1, keepdims=True)
    return centred * lax.rsqrt(variance + norm_eps) * norm_gain + norm_shift


def exact_gelu(inner_pre):
    return jax.nn.gelu(inner_pre, approximate=False)


def matmul(left, right):
    return jnp.dot(left, right, preferred_element_type=f32)


def matmul_nt(left, right):
    return lax.dot_general(left, right, (((1,), (1,)), ((), ())), preferred_element_type=f32)


def matmul_tn(left, right):
    return lax.dot_general(left, right, (((0,), (0,)), ((), ())), preferred_element_type=f32)


def matmul_tt(left, right):
    return lax.dot_general(left, right, (((0,), (1,)), ((), ())), preferred_element_type=f32)


def swap(x, axis, mask):
    size = lax.axis_size(axis)
    return lax.ppermute(x, axis, [(i, i ^ mask) for i in range(size)])


def bits_of(size):
    assert size & (size - 1) == 0
    return [1 << b for b in range(size.bit_length() - 1)]


def gather_axis(x, axis, masks=None):
    index = lax.axis_index(axis)
    out = x[None]
    for mask in masks or bits_of(lax.axis_size(axis)):
        other = swap(out, axis, mask)
        low = (index & mask) == 0
        out = jnp.concatenate([jnp.where(low, out, other), jnp.where(low, other, out)], axis=0)
    return out


def shift(x, axis, step):
    size = lax.axis_size(axis)
    return lax.ppermute(x, axis, [(i, (i + step) % size) for i in range(size)])


def weight_gather(x):
    size = lax.axis_size("ctx")
    index = lax.axis_index("ctx")
    out = jnp.zeros((size,) + x.shape, x.dtype)
    out = lax.dynamic_update_index_in_dim(out, x, index, 0)
    for step in range(1, size):
        out = lax.dynamic_update_index_in_dim(
            out, shift(x, "ctx", step), (index - step) % size, 0
        )
    out = gather_axis(out, "dp")
    return out.reshape(-1, x.shape[1])


def weight_scatter(total):
    dp, ctx = lax.axis_size("dp"), lax.axis_size("ctx")
    own = total.shape[0] // (dp * ctx)
    rest = total
    index = lax.axis_index("dp")
    for mask in reversed(bits_of(dp)):
        halves = rest.reshape(2, rest.shape[0] // 2, rest.shape[1])
        bit = (index & mask) != 0
        home = jnp.where(bit, halves[1], halves[0])
        away = jnp.where(bit, halves[0], halves[1])
        rest = home + swap(away.astype(bf16), "dp", mask).astype(f32)
    rest = rest.reshape(ctx, own, rest.shape[1])
    index = lax.axis_index("ctx")
    low = rest.astype(bf16)
    out = lax.dynamic_index_in_dim(rest, index, 0, keepdims=False)
    for step in range(1, ctx):
        sent = lax.dynamic_index_in_dim(low, (index + step) % ctx, 0, keepdims=False)
        out = out + shift(sent, "ctx", step).astype(f32)
    return out


def tp_gather(x):
    index = lax.axis_index("tp")
    rows, width = x.shape
    far = swap(x, "tp", 2)
    low = (index & 2) == 0
    pair = jnp.concatenate([jnp.where(low, x, far), jnp.where(low, far, x)])
    near = swap(pair, "tp", 1)
    low = (index & 1) == 0
    return jnp.concatenate([jnp.where(low, pair, near), jnp.where(low, near, pair)])


def tp_scatter(part, rows):
    index = lax.axis_index("tp")
    near, far = index & 1, index >> 1
    sent = swap(part(1 - near).astype(bf16), "tp", 1)
    kept = (part(near) + sent.astype(f32)).reshape(2, rows, -1)
    away = lax.dynamic_index_in_dim(kept, 1 - far, axis=0, keepdims=False)
    home = lax.dynamic_index_in_dim(kept, far, axis=0, keepdims=False)
    return home + swap(away.astype(bf16), "tp", 2).astype(f32)


def near_rows(x, which):
    half = x.shape[0] // 2
    return lax.dynamic_slice_in_dim(x, which * half, half, 0)


def near_cols(x, which):
    half = x.shape[1] // 2
    return lax.dynamic_slice_in_dim(x, which * half, half, 1)


def head_mask(width, head, span):
    lane = lax.broadcasted_iota(jnp.int32, (1, width), 1)
    return ((lane >= head * HD) & (lane < head * HD + HD)) | (lane >= span)


def head_lanes(width, head):
    lane = lax.broadcasted_iota(jnp.int32, (1, width), 1)
    return (lane >= head * HD) & (lane < head * HD + HD)


def slot_of(row, own):
    block = row // own
    return ((block & 1) * 2 + (block >> 1)) * own + (row - block * own)


def read_mask(scal_ref, rel, row, count, group_rows, own):
    group = scal_ref[0]
    key = (group - rel) * group_rows + slot_of(
        lax.broadcasted_iota(jnp.int32, (1, group_rows), 1), own
    )
    inside = (key >= 0) & (key < scal_ref[1])
    if rel:
        return inside
    query = group * group_rows + slot_of(
        row * count + lax.broadcasted_iota(jnp.int32, (count, 1), 0), own
    )
    return (key <= query) & inside


def attend_kernel(cfg, chunks, scal_ref, *refs):
    heads, causal, group_rows, own = cfg
    q_ref, kv_refs = refs[0], refs[1 : 1 + chunks]
    o_ref, lse_ref = refs[1 + chunks :]
    span = heads * HD
    width = q_ref.shape[1]

    def row_body(row, carry):
        rows = pl.ds(pl.multiple_of(row * FQ, FQ), FQ)
        q_all = q_ref[rows, :]
        out = jnp.zeros((FQ, span), f32)
        lse_out = jnp.zeros((FQ, 128), f32)
        lane = lax.broadcasted_iota(jnp.int32, (1, 128), 1)
        every = []
        for head in range(heads):
            q_h = q_all * head_mask(width, head, span).astype(bf16)
            parts = []
            for rel, kv_ref in enumerate(kv_refs):
                s = matmul_nt(q_h, kv_ref[:, :width])
                if causal:
                    allowed = read_mask(scal_ref, rel, row, FQ, group_rows, own)
                    s = jnp.where(allowed, s, masked_fill)
                parts.append(s)
            every.append(parts)
        for head in range(heads):
            parts = every[head]
            top = jnp.max(parts[0], axis=1, keepdims=True)
            for s in parts[1:]:
                top = jnp.maximum(top, jnp.max(s, axis=1, keepdims=True))
            acc = None
            for s, kv_ref in zip(parts, kv_refs):
                mixed = matmul(jnp.exp(s - top).astype(bf16), kv_ref[:, width:])
                acc = mixed if acc is None else acc + mixed
            total = acc[:, span : span + 1]
            out = jnp.where(head_lanes(span, head), acc[:, :span] / total, out)
            lse_out = jnp.where(lane == head, top + jnp.log(total), lse_out)
        o_ref[rows, :] = out
        lse_ref[rows, :] = lse_out
        return carry

    lax.fori_loop(0, q_ref.shape[0] // FQ, row_body, 0)


def attend_grad_kernel(
    cfg, rel, scal_ref, q_ref, kv_ref, do_ref, o_ref, lse_ref,
    dq_ref, dkv_ref, dk_scr, dv_scr, dq_scr,
):
    heads, causal, group_rows, own = cfg
    span = heads * HD
    width = q_ref.shape[1]
    tiles = kv_ref.shape[0] // group_rows
    dk_scr[...] = jnp.zeros(dk_scr.shape, f32)
    dv_scr[...] = jnp.zeros(dv_scr.shape, f32)

    def row_body(row, carry):
        rows = pl.ds(pl.multiple_of(row * GQ, GQ), GQ)
        q_all = q_ref[rows, :]
        do_all = do_ref[rows, :]
        q_t = q_all[:, :span].T
        do_t = do_all.T
        prod = do_all.astype(f32) * o_ref[rows, :]
        lse_all = lse_ref[rows, :]
        q_hs, do_hs, deltas = [], [], []
        for head in range(heads):
            keep = head_lanes(span, head)
            q_hs.append(q_all * head_mask(width, head, span).astype(bf16))
            do_hs.append(do_all * keep.astype(bf16))
            deltas.append(jnp.sum(jnp.where(keep, prod, 0.0), axis=1, keepdims=True))
        dq_scr[...] = jnp.zeros(dq_scr.shape, f32)

        def step(tile, inner):
            at = pl.ds(pl.multiple_of(tile * group_rows, group_rows), group_rows)
            k_t = kv_ref[at, :width]
            v_t = kv_ref[at, width : width + span]
            for head in range(heads):
                band = slice(head * HD, head * HD + HD)
                s = matmul_nt(q_hs[head], k_t)
                if causal:
                    allowed = read_mask(scal_ref, rel, row, GQ, group_rows, own)
                    s = jnp.where(allowed, s, masked_fill)
                p = jnp.exp(s - lse_all[:, head : head + 1])
                ds = (p * (matmul_nt(do_hs[head], v_t) - deltas[head])).astype(bf16)
                dv_scr[tile, band, :] += matmul(do_t[band, :], p.astype(bf16))
                dk_scr[tile, band, :] += matmul(q_t[band, :], ds)
                dq_scr[head] += matmul(ds, k_t)
            return inner

        lax.fori_loop(0, tiles, step, 0)
        dq_out = jnp.zeros((GQ, span), f32)
        for head in range(heads):
            dq_out = jnp.where(head_lanes(span, head), dq_scr[head][:, :span], dq_out)
        dq_ref[rows, :] = dq_out.astype(dq_ref.dtype)
        return carry

    def run():
        lax.fori_loop(0, q_ref.shape[0] // GQ, row_body, 0)

    if causal and rel:

        @pl.when(scal_ref[0] >= rel)
        def _():
            run()

        @pl.when(scal_ref[0] < rel)
        def _():
            dq_ref[...] = jnp.zeros(dq_ref.shape, dq_ref.dtype)

    else:
        run()
    for tile in range(tiles):
        dkv_ref[tile, 0:span, :] = dk_scr[tile].astype(bf16)
        dkv_ref[tile, span : 2 * span, :] = dv_scr[tile].astype(bf16)


def smem():
    return pl.BlockSpec(memory_space=pltpu.SMEM)


def vmem():
    return pl.BlockSpec(memory_space=pltpu.VMEM)


def attend(cfg, scal, q, chunks):
    span = cfg[0] * HD
    rows = q.shape[0]
    return pl.pallas_call(
        functools.partial(attend_kernel, cfg, len(chunks)),
        out_shape=(
            jax.ShapeDtypeStruct((rows, span), f32),
            jax.ShapeDtypeStruct((rows, 128), f32),
        ),
        in_specs=[smem()] + [vmem()] * (1 + len(chunks)),
        out_specs=(vmem(), vmem()),
        name="attend",
    )(scal, q, *chunks)


def attend_grad(cfg, rel, scal, q, kv, do, o, lse, dq_type):
    heads, _, group_rows, _ = cfg
    rows, span = q.shape[0], heads * HD
    tiles = kv.shape[0] // group_rows
    return pl.pallas_call(
        functools.partial(attend_grad_kernel, cfg, rel),
        out_shape=(
            jax.ShapeDtypeStruct((rows, span), dq_type),
            jax.ShapeDtypeStruct((tiles, 2 * span, group_rows), bf16),
        ),
        in_specs=[smem()] + [vmem()] * 5,
        out_specs=(vmem(), vmem()),
        scratch_shapes=[
            pltpu.VMEM((tiles, span, group_rows), f32),
            pltpu.VMEM((tiles, span, group_rows), f32),
            pltpu.VMEM((heads, GQ, q.shape[1]), f32),
        ],
        name="attend_grad",
    )(scal, q, kv, do, o, lse)


def per_device(
    tokens,
    enc_states,
    chosen_blocks,
    seq_lengths,
    cotangent,
    self_query,
    self_key,
    self_value,
    self_output,
    cross_query,
    cross_key,
    cross_value,
    cross_output,
    ffn_inner,
    ffn_outer,
    query_bias,
    value_bias,
    output_bias,
    cquery_bias,
    cvalue_bias,
    coutput_bias,
    inner_bias,
    outer_bias,
    norm1_gain,
    norm1_shift,
    norm2_gain,
    norm2_shift,
    norm3_gain,
    norm3_shift,
):
    tp_count = lax.axis_size("tp")
    ctx_count = lax.axis_size("ctx")
    dp_count = lax.axis_size("dp")
    head_slot = lax.axis_index("tp")
    group_slot = lax.axis_index("ctx")
    assert tp_count == 4
    columns = self_query.shape[1]
    hidden_cols = ffn_inner.shape[1]
    heads = columns // HD
    both = 2 * columns

    spare = WIDE - columns
    block_count = enc_states.shape[1] * ctx_count // BLK
    assert columns + block_count <= WIDE and spare > 0

    self_full = weight_gather(
        jnp.concatenate([self_key, self_value, self_query, self_output], axis=1)
    )
    cross_full = lax.all_gather(
        jnp.concatenate([cross_key, cross_value, cross_query, cross_output], axis=1),
        ("dp", "ctx"),
        axis=0,
        tiled=True,
    )
    ffn_full = lax.all_gather(
        jnp.concatenate([ffn_inner, ffn_outer], axis=1), ("dp", "ctx"), axis=0, tiled=True
    )

    def widened(matrix):
        return jnp.pad(matrix, ((0, 0), (0, spare)))

    skv_full, query_full, output_full = (
        jnp.concatenate(
            [widened(self_full[:, :columns]), widened(self_full[:, columns:both])], axis=1
        ),
        self_full[:, both : 3 * columns],
        self_full[:, 3 * columns :],
    )
    ckv_full, cquery_full, coutput_full = (
        cross_full[:, :both],
        cross_full[:, both : 3 * columns],
        cross_full[:, 3 * columns :],
    )
    inner_full, outer_full = ffn_full[:, :hidden_cols], ffn_full[:, hidden_cols:]

    vectors = (
        query_bias, value_bias, output_bias, cquery_bias, cvalue_bias, coutput_bias, inner_bias,
        outer_bias, norm1_gain, norm1_shift, norm2_gain, norm2_shift, norm3_gain, norm3_shift,
    )
    sizes = [vector.shape[0] for vector in vectors]
    packed = jnp.concatenate(vectors)
    packed_size = packed.shape[0]
    members = dp_count * ctx_count * tp_count
    spread = packed[None, :]
    spread = gather_axis(spread, "tp", [1, 2])
    spread = gather_axis(spread.reshape(1, tp_count, packed_size), "ctx")
    spread = gather_axis(spread.reshape(1, ctx_count * tp_count, packed_size), "dp")
    spread = spread.reshape(members, packed_size)
    full_vectors = []
    at = 0
    for size in sizes:
        full_vectors.append(spread[:, at : at + size].reshape(members * size))
        at += size
    (
        query_vec, value_vec, output_vec, cquery_vec, cvalue_vec, coutput_vec, inner_vec,
        outer_vec, gain_one, shift_one, gain_two, shift_two, gain_three, shift_three,
    ) = full_vectors

    def local_cols(vector, width):
        return lax.dynamic_slice_in_dim(vector, head_slot * width, width, 0)

    def placed(local_sum, full_width):
        return lax.dynamic_update_slice_in_dim(
            jnp.zeros((full_width,), f32), local_sum, head_slot * local_sum.shape[0], 0
        )

    def widen_vec(vector):
        return jnp.pad(vector, (0, spare))

    def rows_product(mixed, weight_full):
        return lambda which: matmul_nt(near_rows(mixed, which), weight_full)

    def value_half(vector):
        return jnp.concatenate([jnp.zeros((columns,), f32), local_cols(vector, columns)])

    token_rows = tokens[0]
    own_rows, width = token_rows.shape
    group_rows = own_rows * tp_count
    seq_total = group_rows * ctx_count
    enc_group = enc_states.shape[1]
    enc_total = enc_group * ctx_count
    length = seq_lengths[0]
    own_pos = group_slot * group_rows + head_slot * own_rows + jnp.arange(own_rows)
    row_valid = (own_pos < length).astype(f32)[:, None]
    scal = jnp.stack([group_slot.astype(jnp.int32), length.astype(jnp.int32)])

    right = [(i, i + 1) for i in range(ctx_count - 1)]
    left = [(i + 1, i) for i in range(ctx_count - 1)]
    held, token_groups = token_rows, [tp_gather(token_rows)]
    for _ in range(ctx_count - 1):
        held = lax.ppermute(held, "ctx", right)
        token_groups.append(tp_gather(held))
    complete_rows = token_groups[0]
    ones = jnp.ones((1,), f32)
    kv_bias = jnp.concatenate(
        [jnp.zeros((WIDE,), f32), local_cols(value_vec, columns), ones, jnp.zeros((spare - 1,), f32)]
    )
    kv_groups = [(matmul(rows, skv_full) + kv_bias).astype(bf16) for rows in token_groups]
    self_queries = (
        (matmul(complete_rows, widened(query_full)) + widen_vec(local_cols(query_vec, columns)))
        * 0.125
    ).astype(bf16)
    self_cfg = (heads, True, group_rows, own_rows)

    state_rows = enc_states[0]
    enc_kv = (matmul(state_rows, ckv_full) + value_half(cvalue_vec)).astype(bf16)
    all_enc_kv = lax.all_gather(enc_kv, "ctx", axis=0, tiled=True)
    block_of = lax.broadcasted_iota(jnp.int32, (enc_total, spare), 0) // BLK
    hot = (block_of == lax.broadcasted_iota(jnp.int32, (enc_total, spare), 1)).astype(bf16)
    enc_wide = jnp.concatenate(
        [
            all_enc_kv[:, :columns],
            hot,
            all_enc_kv[:, columns:],
            jnp.ones((enc_total, spare), bf16),
        ],
        axis=1,
    )
    picked = lax.dynamic_slice_in_dim(chosen_blocks[0], group_slot * group_rows, group_rows, 0)
    picked = picked.reshape(2, 2, own_rows, -1).swapaxes(0, 1).reshape(group_rows, -1)
    hit = jnp.any(picked[:, :, None] == jnp.arange(spare)[None, None, :], axis=1)
    known = hit | (jnp.arange(spare) >= block_count)[None, :]
    block_fill = jnp.pad(jnp.where(known, 0.0, masked_fill), ((0, 0), (columns, 0)))
    cross_cfg = (heads, False, enc_group, own_rows)

    self_mix, self_lse = attend(self_cfg, scal, self_queries, kv_groups)
    self_mixed = self_mix.astype(bf16)
    resid_one = (
        token_rows.astype(f32)
        + tp_scatter(rows_product(self_mixed, output_full), own_rows)
        + output_vec
    )
    hidden_one, pull_one = jax.vjp(layer_norm, resid_one, gain_one, shift_one)
    rows_one = tp_gather(hidden_one.astype(bf16))
    cross_q = (
        (matmul(rows_one, widened(cquery_full)) + widen_vec(local_cols(cquery_vec, columns))) * 0.125
        + block_fill
    ).astype(bf16)
    cross_mix, cross_lse = attend(cross_cfg, scal, cross_q, [enc_wide])
    cross_mixed = cross_mix.astype(bf16)
    resid_two = hidden_one + tp_scatter(rows_product(cross_mixed, coutput_full), own_rows) + coutput_vec
    hidden_two, pull_two = jax.vjp(layer_norm, resid_two, gain_two, shift_two)
    rows_two = tp_gather(hidden_two.astype(bf16))
    inner_pre = matmul(rows_two, inner_full) + local_cols(inner_vec, hidden_cols)
    activated_full, pull_gelu = jax.vjp(exact_gelu, inner_pre)
    activated = activated_full.astype(bf16)
    resid_three = hidden_two + tp_scatter(rows_product(activated, outer_full), own_rows) + outer_vec
    hidden_three, pull_three = jax.vjp(layer_norm, resid_three, gain_three, shift_three)
    output = (hidden_three * row_valid).astype(bf16)

    def scatter_weights(*parts):
        return lax.psum_scatter(
            jnp.concatenate([part.astype(bf16) for part in parts], axis=1),
            ("dp", "ctx"),
            scatter_dimension=0,
            tiled=True,
        ).astype(f32)

    grad_resid3, grad_gain3, grad_shift3 = pull_three(cotangent[0].astype(f32) * row_valid)
    ffn_grad_rows = tp_gather(grad_resid3.astype(bf16))
    act_grad = matmul(ffn_grad_rows, outer_full)
    (inner_grad_full,) = pull_gelu(act_grad)
    inner_grad = inner_grad_full.astype(bf16)
    grad_hidden2 = grad_resid3 + tp_scatter(rows_product(inner_grad, inner_full), own_rows)
    ffn_part = scatter_weights(
        matmul_tn(rows_two, inner_grad), matmul_tn(ffn_grad_rows, activated)
    )
    inner_bgrad = placed(jnp.sum(inner_grad, axis=0, dtype=f32), inner_vec.shape[0])
    outer_bgrad = jnp.sum(grad_resid3, axis=0)
    grad_resid2, grad_gain2, grad_shift2 = pull_two(grad_hidden2)
    cross_grad_rows = tp_gather(grad_resid2.astype(bf16))
    cross_mixed_grad = matmul(cross_grad_rows, coutput_full).astype(bf16)
    coutput_bgrad = jnp.sum(grad_resid2, axis=0)
    cross_query_grad, cross_kv_part = attend_grad(
        cross_cfg, 0, scal, cross_q, enc_wide, cross_mixed_grad, cross_mix, cross_lse, bf16
    )
    grad_hidden1 = grad_resid2 + 0.125 * tp_scatter(
        rows_product(cross_query_grad, cquery_full), own_rows
    )
    enc_grad_t = lax.psum_scatter(cross_kv_part, "ctx", scatter_dimension=0, tiled=False)
    cross_part = scatter_weights(
        matmul_tt(state_rows, enc_grad_t),
        0.125 * matmul_tn(rows_one, cross_query_grad),
        matmul_tn(cross_grad_rows, cross_mixed),
    )
    cquery_bgrad = placed(0.125 * jnp.sum(cross_query_grad, axis=0, dtype=f32), width)
    cvalue_bgrad = placed(jnp.sum(enc_grad_t[columns:], axis=1, dtype=f32), width)
    state_split = enc_grad_t.reshape(both, 2, 2, enc_group // 4).swapaxes(1, 2)
    state_split = state_split.reshape(both, enc_group)
    state_grad = tp_scatter(
        lambda which: matmul_tt(near_cols(state_split, which), ckv_full), enc_group // 4
    ).astype(bf16)
    grad_resid1, grad_gain1, grad_shift1 = pull_one(grad_hidden1)
    self_grad_rows = tp_gather(grad_resid1.astype(bf16))
    self_mixed_grad = matmul(self_grad_rows, output_full).astype(bf16)
    output_bgrad = jnp.sum(grad_resid1, axis=0)
    moved, squery_sum, skv_wgrad, value_bgrad = None, None, None, None
    for rel in reversed(range(ctx_count)):
        squery_part, kv_part = attend_grad(
            self_cfg, rel, scal, self_queries, kv_groups[rel], self_mixed_grad, self_mix, self_lse,
            f32,
        )
        kv_part = kv_part[0]
        squery_sum = squery_part if squery_sum is None else squery_sum + squery_part
        wgrad = matmul_tt(token_groups[rel], kv_part)
        skv_wgrad = wgrad if skv_wgrad is None else skv_wgrad + wgrad
        bgrad = jnp.sum(kv_part[columns:], axis=1, dtype=f32)
        value_bgrad = bgrad if value_bgrad is None else value_bgrad + bgrad
        moved = kv_part if moved is None else (kv_part.astype(f32) + moved.astype(f32)).astype(bf16)
        if rel:
            moved = lax.ppermute(moved, "ctx", left)
    squery_grad = squery_sum.astype(bf16)
    self_part = weight_scatter(
        jnp.concatenate(
            [
                skv_wgrad,
                0.125 * matmul_tn(complete_rows, squery_grad),
                matmul_tn(self_grad_rows, self_mixed),
            ],
            axis=1,
        )
    )
    query_bgrad = placed(0.125 * jnp.sum(squery_grad, axis=0, dtype=f32), width)
    value_bgrad = placed(value_bgrad, width)
    token_grad = grad_resid1 + tp_scatter(
        lambda which: 0.125 * matmul_nt(near_rows(squery_grad, which), query_full)
        + matmul_tt(near_cols(moved, which), self_full[:, :both]),
        own_rows,
    )

    vector_sums = (
        query_bgrad, value_bgrad, output_bgrad, cquery_bgrad, cvalue_bgrad, coutput_bgrad,
        inner_bgrad, outer_bgrad, grad_gain1, grad_shift1, grad_gain2, grad_shift2, grad_gain3,
        grad_shift3,
    )
    folded = jnp.concatenate(
        [vector.reshape(members, size) for vector, size in zip(vector_sums, sizes)], axis=1
    )
    for axis in ("dp", "ctx", "tp"):
        index = lax.axis_index(axis)
        for mask in reversed(bits_of(lax.axis_size(axis))):
            halves = folded.reshape(2, folded.shape[0] // 2, packed_size)
            bit = (index & mask) != 0
            home = jnp.where(bit, halves[1], halves[0])
            away = jnp.where(bit, halves[0], halves[1])
            folded = home + swap(away, axis, mask)
    own_vectors = folded.reshape(packed_size)
    vector_grads = []
    at = 0
    for size in sizes:
        vector_grads.append(own_vectors[at : at + size])
        at += size

    def cols(part, start, stop):
        return part[:, start * columns : stop * columns]

    weight_grads = (
        cols(self_part, 2, 3), cols(self_part, 0, 1), cols(self_part, 1, 2), cols(self_part, 3, 4),
        cols(cross_part, 2, 3), cols(cross_part, 0, 1), cols(cross_part, 1, 2),
        cols(cross_part, 3, 4), ffn_part[:, :hidden_cols], ffn_part[:, hidden_cols:],
    )
    return (
        (output[None], token_grad.astype(bf16)[None], state_grad[None])
        + weight_grads
        + tuple(vector_grads)
    )


def solution(mesh):
    in_specs = (
        P("dp", ("ctx", "tp"), None),
        P("dp", "ctx", None),
        P("dp", None, None),
        P("dp"),
        P("dp", ("ctx", "tp"), None),
        P(("dp", "ctx"), "tp"),
        P(("dp", "ctx"), "tp"),
        P(("dp", "ctx"), "tp"),
        P(("dp", "ctx"), "tp"),
        P(("dp", "ctx"), "tp"),
        P(("dp", "ctx"), "tp"),
        P(("dp", "ctx"), "tp"),
        P(("dp", "ctx"), "tp"),
        P(("dp", "ctx"), "tp"),
        P(("dp", "ctx"), "tp"),
        P(("dp", "ctx", "tp")),
        P(("dp", "ctx", "tp")),
        P(("dp", "ctx", "tp")),
        P(("dp", "ctx", "tp")),
        P(("dp", "ctx", "tp")),
        P(("dp", "ctx", "tp")),
        P(("dp", "ctx", "tp")),
        P(("dp", "ctx", "tp")),
        P(("dp", "ctx", "tp")),
        P(("dp", "ctx", "tp")),
        P(("dp", "ctx", "tp")),
        P(("dp", "ctx", "tp")),
        P(("dp", "ctx", "tp")),
        P(("dp", "ctx", "tp")),
    )
    out_specs = (
        P("dp", ("ctx", "tp"), None),
        P("dp", ("ctx", "tp"), None),
        P("dp", ("ctx", "tp"), None),
        P(("dp", "ctx"), "tp"),
        P(("dp", "ctx"), "tp"),
        P(("dp", "ctx"), "tp"),
        P(("dp", "ctx"), "tp"),
        P(("dp", "ctx"), "tp"),
        P(("dp", "ctx"), "tp"),
        P(("dp", "ctx"), "tp"),
        P(("dp", "ctx"), "tp"),
        P(("dp", "ctx"), "tp"),
        P(("dp", "ctx"), "tp"),
        P(("dp", "ctx", "tp")),
        P(("dp", "ctx", "tp")),
        P(("dp", "ctx", "tp")),
        P(("dp", "ctx", "tp")),
        P(("dp", "ctx", "tp")),
        P(("dp", "ctx", "tp")),
        P(("dp", "ctx", "tp")),
        P(("dp", "ctx", "tp")),
        P(("dp", "ctx", "tp")),
        P(("dp", "ctx", "tp")),
        P(("dp", "ctx", "tp")),
        P(("dp", "ctx", "tp")),
        P(("dp", "ctx", "tp")),
        P(("dp", "ctx", "tp")),
    )
    return jax.shard_map(
        per_device, mesh=mesh, in_specs=in_specs, out_specs=out_specs, check_vma=False
    )
```
